128 devices in a mesh: sensor: 16 (over y, z_lo, core), channel: 4 (over x), tm: 2 (over z_hi).
Axes of the slice: x: 4, y: 4, z: 4 (z_hi: 2, z_lo: 2; z = z_hi * 2 + z_lo), core: 2. Of those that a mesh axis runs over, the one named last changes fastest.
Arguments:
- tensor: float32 [12288, 128, 512], P('sensor', 'tm', 'channel'), may hold values from -6 to 6
- core: float32 [64, 64, 32], replicated, may hold values from -0.015625 to 0.015625
- sensor_factor: float32 [12288, 64], P('sensor'), may hold values from -6 to 6
- channel_factor: float32 [512, 64], P('channel'), may hold values from -6 to 6
- time_factor: float32 [128, 32], P('tm'), may hold values from -6 to 6
- neighbour_ids: int32 [96, 4], P('sensor'), may hold values from 0 to 95
- edge_weights: int32 [96, 4, 128, 128], P('sensor'), may hold values from 0 to 3
Outputs:
- core_grad: float32 [64, 64, 32], replicated
- sensor_grad: float32 [12288, 64], P(('sensor', 'channel', 'tm'))
- channel_grad: float32 [512, 64], P('channel')
- time_grad: float32 [128, 32], P('tm')
The draws below stay inside these ranges and needn't reach their ends.
All inputs are finite; a program needn't handle non-finite values.
Results may differ from the reference program's by a relative error of at most 0.0001.
Values sent between devices are 32-bit elements; how exact they have to be, the bound alone decides.
A program may use at most 192 MiB of HBM per device.

```python
import math
import jax
import jax.numpy as jnp
from jax import lax

CHANNELS = 512
R1 = 64
R2 = 64
R3 = 32
BLOCK = 128
NBR = 4
SENSORS = 12288
TIME = 128
BLOCKS = 96


def plant(array, own_key, low, top_value):
    longest = array.shape.index(max(array.shape))
    spots = []
    for shift in (0, 1):
        where = [jax.random.randint(jax.random.fold_in(own_key, axis), (), 0, length) for axis, length in enumerate(array.shape)]
        where[longest] = (where[longest] + shift) % array.shape[longest]
        spots.append(tuple(where))
    return array.at[spots[0]].set(low).at[spots[1]].set(top_value)


def shard_levels(rng, shape, cuts, low, top_value):
    def one(axis_at, shards_of):
        draws = jax.random.uniform(jax.random.fold_in(jax.random.fold_in(rng, 6), axis_at), (shards_of,), jnp.float32, low / len(cuts), top_value / len(cuts))
        return jnp.repeat(jnp.exp(draws), shape[axis_at] // shards_of).reshape((-1,) + (1,) * (len(shape) - axis_at - 1))

    level = one(*cuts[0])
    for cut in cuts[1:]:
        level = level * one(*cut)
    return level


def scatter_about(rng, shape, spread, reach, shards=(), kind=jnp.bfloat16):
    level = shard_levels(rng, shape, shards, -0.22, 0.18) if shards else 1.0
    result = jax.random.normal(rng, shape, jnp.float32) * spread * level
    return jnp.minimum(jnp.maximum(result, -reach), reach).astype(kind)


def setup_inputs(seed: int = 0) -> dict:
    keys = jax.random.split(jax.random.key(seed), 8)
    return {
        "tensor": scatter_about(keys[0], (SENSORS, TIME, CHANNELS), 1.0, 6.0, ((0, 16), (1, 2), (2, 4)), jnp.float32),
        "core": scatter_about(keys[1], (R1, R2, R3), (R1 * R2 * R3) ** -0.5, 0.015625, (), jnp.float32),
        "sensor_factor": scatter_about(keys[2], (SENSORS, R1), 1.0, 6.0, ((0, 16),), jnp.float32),
        "channel_factor": scatter_about(keys[3], (CHANNELS, R2), 1.0, 6.0, ((0, 4),), jnp.float32),
        "time_factor": scatter_about(keys[4], (TIME, R3), 1.0, 6.0, ((0, 2),), jnp.float32),
        "neighbour_ids": plant(jax.random.randint(keys[5], (BLOCKS, NBR), 0, BLOCKS), jax.random.fold_in(keys[5], 1), 0, BLOCKS - 1).astype(jnp.int32),
        "edge_weights": plant(jax.random.randint(keys[6], (BLOCKS, NBR, BLOCK, BLOCK), 0, 4), jax.random.fold_in(keys[6], 1), 0, 3).astype(jnp.int32),
    }


lap_weight = 1.0 / 512.0
highest = lax.Precision.HIGHEST

def reference(tensor, core, sensor_factor, channel_factor, time_factor, neighbour_ids, edge_weights):
    core_time = jnp.einsum('rst,kt->rks', core, time_factor, precision=highest)
    core_both = jnp.einsum('rks,js->rkj', core_time, channel_factor, precision=highest)
    core_chan = jnp.einsum('rst,js->rtj', core, channel_factor, precision=highest)
    flat_core = core_both.reshape(R1, TIME * CHANNELS)

    def accumulate(running, pieces):
        tensor_block, factor_block = pieces
        residual = jnp.dot(factor_block, flat_core, precision=highest) - tensor_block.reshape(BLOCK, TIME * CHANNELS)
        folded = jnp.dot(factor_block.T, residual, precision=highest)
        fit_block = jnp.dot(residual, flat_core.T, precision=highest)
        return (running + folded, fit_block)
    start = jnp.zeros((R1, TIME * CHANNELS), jnp.float32)
    folded_total, fit_rows = lax.scan(accumulate, start, (tensor.reshape(BLOCKS, BLOCK, TIME, CHANNELS), sensor_factor.reshape(BLOCKS, BLOCK, R1)))
    folded3 = folded_total.reshape(R1, TIME, CHANNELS)
    inner = jnp.einsum('rkj,js->rks', folded3, channel_factor, precision=highest)
    core_grad = jnp.einsum('rks,kt->rst', inner, time_factor, precision=highest) / math.sqrt(SENSORS * TIME * CHANNELS)
    channel_grad = jnp.einsum('rkj,rks->js', folded3, core_time, precision=highest) / math.sqrt(SENSORS * TIME)
    time_grad = jnp.einsum('rkj,rtj->kt', folded3, core_chan, precision=highest) / math.sqrt(SENSORS * CHANNELS)
    fit = fit_rows.reshape(SENSORS, R1) / math.sqrt(TIME * CHANNELS)
    weights_float = edge_weights.astype(jnp.float32)
    blocks_all = sensor_factor.reshape(BLOCKS, BLOCK, R1)
    neighbours = blocks_all[neighbour_ids]
    pulled = jnp.einsum('bnic,bncd->bid', weights_float, neighbours, precision=highest)
    degree = lax.optimization_barrier(jnp.sum(weights_float, axis=(1, 3)))
    graph_term = lap_weight * (degree[:, :, None] * blocks_all - pulled)
    sensor_grad = fit + graph_term.reshape(SENSORS, R1)
    return (core_grad, sensor_grad, channel_grad, time_grad)
```

```python
import functools
import math

import jax
import jax.numpy as jnp
from jax import lax
from jax.experimental import pallas as pl
from jax.experimental.pallas import tpu as pltpu
from jax.sharding import PartitionSpec as P

lap_weight = 1.0 / 512.0
high = lax.Precision.HIGH
highest = lax.Precision.HIGHEST
f32 = jnp.float32
bf16 = jnp.bfloat16
AXES = ("sensor", "channel", "tm")


def split(value):
    top = value.astype(bf16)
    return top, (value - top.astype(f32)).astype(bf16)


def slab(steps, tensor_ref, rows_ref, chan_ref, ct_ref, folded_ref, fit_ref, fold_lhs, chan_lhs, square_lhs, fit_sum, gram):
    step = pl.program_id(0)
    sensors, slab_steps, chans = tensor_ref.shape
    rank = rows_ref.shape[0]

    @pl.when(step == 0)
    def _():
        rows = rows_ref[...]
        top, low = split(rows)
        fold_lhs[0:rank, 0:sensors] = top
        fold_lhs[0:rank, sensors:] = top
        fold_lhs[rank:, 0:sensors] = low
        fold_lhs[rank:, sensors:] = jnp.zeros_like(low)
        square = lax.dot_general(rows, rows, (((1,), (1,)), ((), ())), precision=highest, preferred_element_type=f32)
        top, low = split(square)
        square_lhs[...] = jnp.concatenate([top, top, low, jnp.zeros_like(low)], axis=1)
        top, low = split(chan_ref[...].T)
        chan_lhs[...] = jnp.concatenate([top, low, top], axis=1)
        fit_sum[...] = jnp.zeros_like(fit_sum)
        gram[...] = jnp.zeros_like(gram)

    flat = tensor_ref.reshape(sensors * slab_steps, chans)
    model = jnp.dot(chan_lhs[...], ct_ref[...], preferred_element_type=f32)
    lower_half = lax.broadcasted_iota(jnp.int32, (chans, 2 * rank), 1) < rank
    for pair in range(slab_steps // 2):
        wide, narrow = [], []
        for k in (2 * pair, 2 * pair + 1):
            piece = model[:, k * 2 * rank : (k + 1) * 2 * rank]
            top = piece.astype(bf16).astype(f32)
            wide.append(jnp.where(lower_half, top, piece - top).astype(bf16))
            narrow.append(jnp.where(lower_half, top, 0.0).astype(bf16))
        both = jnp.concatenate(wide, axis=0)
        first = jnp.concatenate(narrow, axis=0)
        data = jnp.concatenate(
            [flat[pl.ds(2 * pair, sensors, stride=slab_steps), :], flat[pl.ds(2 * pair + 1, sensors, stride=slab_steps), :]], axis=1
        )
        top, low = split(data)
        part = jnp.dot(fold_lhs[...], jnp.concatenate([top, low], axis=0), preferred_element_type=f32)
        own = lax.dot_general(
            square_lhs[...], jnp.concatenate([both, first], axis=1), (((1,), (1,)), ((), ())), preferred_element_type=f32
        )
        total = own - (part[:rank] + part[rank:])
        folded_ref[:, 2 * pair, :] = total[:, :chans]
        folded_ref[:, 2 * pair + 1, :] = total[:, chans:]
        fit_sum[...] += jnp.dot(
            jnp.concatenate([top, low], axis=1), jnp.concatenate([both, first], axis=0), preferred_element_type=f32
        )
        gram[...] += lax.dot_general(both, both, (((0,), (0,)), ((), ())), preferred_element_type=f32)

    @pl.when(step == steps - 1)
    def _():
        grams = gram[...]
        left = grams[:rank] + grams[rank:]
        square = left[:, :rank] + left[:, rank:]
        seen = fit_sum[...]
        model_fit = lax.dot_general(
            rows_ref[...], square, (((0,), (0,)), ((), ())), precision=highest, preferred_element_type=f32
        )
        fit_ref[...] = model_fit - (seen[:, :rank] + seen[:, rank:])


def big_pass(tensor, rows, chan, ct, slab_steps=8):
    sensors, times, chans = tensor.shape
    rank = rows.shape[0]
    rank_two = chan.shape[0]
    steps = times // slab_steps
    return pl.pallas_call(
        functools.partial(slab, steps),
        grid=(steps,),
        in_specs=[
            pl.BlockSpec((sensors, slab_steps, chans), lambda i: (0, i, 0)),
            pl.BlockSpec((rank, sensors), lambda i: (0, 0)),
            pl.BlockSpec((rank_two, chans), lambda i: (0, 0)),
            pl.BlockSpec((3 * rank_two, slab_steps * 2 * rank), lambda i: (0, i)),
        ],
        out_specs=[
            pl.BlockSpec((rank, slab_steps, chans), lambda i: (0, i, 0)),
            pl.BlockSpec((sensors, rank), lambda i: (0, 0)),
        ],
        out_shape=[jax.ShapeDtypeStruct((rank, times, chans), f32), jax.ShapeDtypeStruct((sensors, rank), f32)],
        scratch_shapes=[
            pltpu.VMEM((2 * rank, 2 * sensors), bf16),
            pltpu.VMEM((chans, 3 * rank_two), bf16),
            pltpu.VMEM((rank, 4 * rank), bf16),
            pltpu.VMEM((sensors, 2 * rank), f32),
            pltpu.VMEM((2 * rank, 2 * rank), f32),
        ],
        compiler_params=pltpu.CompilerParams(vmem_limit_bytes=50 * 2**20),
        cost_estimate=pl.CostEstimate(flops=8 * 10**9, bytes_accessed=32 * 2**20, transcendentals=0),
    )(tensor, rows, chan, ct)


def on_device(
    tensor, core, sensor_factor, channel_factor, time_factor, neighbour_ids, edge_weights
):
    sensor_rows, time_rows, chan_rows = tensor.shape
    rank_one, rank_two, rank_three = core.shape
    n_sensor = lax.axis_size("sensor")
    n_channel = lax.axis_size("channel")
    n_time = lax.axis_size("tm")
    total_sensors = sensor_rows * n_sensor
    total_time = time_rows * n_time
    total_chan = chan_rows * n_channel
    groups = n_channel * n_time
    chan_index = lax.axis_index("channel")
    time_index = lax.axis_index("tm")
    share_index = chan_index * n_time + time_index
    share = sensor_rows // groups
    block, slots = edge_weights.shape[-1], edge_weights.shape[1]
    blocks = edge_weights.shape[0]

    rows = sensor_factor.T
    block_rows = rows.reshape(rank_one, blocks, block).transpose(1, 0, 2)
    whole_rows = lax.all_gather(block_rows, "sensor", axis=0, tiled=True)

    core_time = jnp.einsum("rst,kt->skr", core, time_factor, precision=highest)
    twice = jnp.concatenate([core_time, core_time], axis=2).reshape(rank_two, time_rows * 2 * rank_one)
    top = lax.reduce_precision(twice, 8, 7)
    ct = jnp.concatenate([top, top, twice - top], axis=0).astype(bf16)
    folded3, fit = big_pass(tensor, rows, channel_factor.T, ct)

    pairs = blocks * slots // groups
    first = share_index * pairs
    weights = lax.dynamic_slice_in_dim(edge_weights.reshape(blocks * slots, block, block), first, pairs, 0).astype(f32)
    ids = lax.dynamic_slice_in_dim(neighbour_ids.reshape(blocks * slots), first, pairs, 0)
    near = jnp.stack([lax.dynamic_index_in_dim(whole_rows, ids[q], 0, keepdims=False) for q in range(pairs)])
    pulled = jnp.einsum("qac,qdc->qad", weights, near, precision=high)
    degree = jnp.sum(weights, axis=2)
    owner = (first + jnp.arange(pairs)) // slots
    chosen = (jnp.arange(blocks)[:, None] == owner[None, :]).astype(f32)
    degrees = jnp.sum(chosen[:, :, None] * degree[None], axis=1).reshape(sensor_rows)
    pulls = jnp.sum(chosen[:, :, None, None] * pulled[None], axis=1).reshape(sensor_rows, rank_one)
    fit_part = fit / math.sqrt(total_time * total_chan) + lap_weight * (degrees[:, None] * sensor_factor - pulls)
    sensor_grad = lax.psum_scatter(fit_part, ("channel", "tm"), scatter_dimension=0, tiled=True)

    inner = jnp.einsum("rkj,js->rks", folded3, channel_factor, precision=high)
    core_part = jnp.einsum("rks,kt->rts", inner, time_factor, precision=high)
    chan_part = jnp.einsum("rkj,skr->sj", folded3, core_time, precision=high)
    time_part = jnp.einsum("rks,rst->tk", inner, core, precision=high)
    chan_slots = jnp.where((jnp.arange(n_channel) == chan_index)[:, None, None], chan_part[None], 0.0)
    time_slots = jnp.where((jnp.arange(n_time) == time_index)[:, None, None], time_part[None], 0.0)
    packed = jnp.concatenate(
        [core_part.reshape(-1, 128), chan_slots.reshape(-1, 128), time_slots.reshape(-1, 128)], axis=0
    )
    total = lax.psum(packed, AXES)
    n_core = core_part.size // 128
    n_chan = n_channel * chan_part.size // 128
    core_grad = total[:n_core].reshape(rank_one, rank_three, rank_two).transpose(0, 2, 1)
    chan_all = total[n_core : n_core + n_chan].reshape(n_channel, rank_two, chan_rows)
    time_all = total[n_core + n_chan :].reshape(n_time, rank_three, time_rows)
    channel_grad = lax.dynamic_index_in_dim(chan_all, chan_index, 0, keepdims=False).T
    time_grad = lax.dynamic_index_in_dim(time_all, time_index, 0, keepdims=False).T
    return (
        core_grad / math.sqrt(total_sensors * total_time * total_chan),
        sensor_grad,
        channel_grad / math.sqrt(total_sensors * total_time),
        time_grad / math.sqrt(total_sensors * total_chan),
    )


def solution(mesh):
    return jax.shard_map(
        on_device,
        mesh=mesh,
        in_specs=(
            P("sensor", "tm", "channel"),
            P(),
            P("sensor", None),
            P("channel", None),
            P("tm", None),
            P("sensor", None),
            P("sensor", None, None, None),
        ),
        out_specs=(P(), P(("sensor", "channel", "tm"), None), P("channel", None), P("tm", None)),
        check_vma=False,
    )
```

```python
import functools
import math

import jax
import jax.numpy as jnp
from jax import lax
from jax.experimental import pallas as pl
from jax.experimental.pallas import tpu as pltpu
from jax.sharding import PartitionSpec as P

lap_weight = 1.0 / 512.0
high = lax.Precision.HIGH
highest = lax.Precision.HIGHEST
f32 = jnp.float32
bf16 = jnp.bfloat16


def split(value):
    top = value.astype(bf16)
    return top, (value - top.astype(f32)).astype(bf16)


def slab(steps, tensor_ref, rows_ref, chan_ref, ct_ref, folded_ref, fit_ref, fold_lhs, chan_lhs, square_lhs, fit_sum, gram):
    step = pl.program_id(0)
    sensors, slab_steps, chans = tensor_ref.shape
    rank = rows_ref.shape[0]

    @pl.when(step == 0)
    def _():
        rows = rows_ref[...]
        top, low = split(rows)
        fold_lhs[0:rank, 0:sensors] = top
        fold_lhs[0:rank, sensors:] = top
        fold_lhs[rank:, 0:sensors] = low
        fold_lhs[rank:, sensors:] = jnp.zeros_like(low)
        square = lax.dot_general(rows, rows, (((1,), (1,)), ((), ())), precision=highest, preferred_element_type=f32)
        top, low = split(square)
        square_lhs[...] = jnp.concatenate([top, top, low, jnp.zeros_like(low)], axis=1)
        top, low = split(chan_ref[...].T)
        chan_lhs[...] = jnp.concatenate([top, low, top], axis=1)
        fit_sum[...] = jnp.zeros_like(fit_sum)
        gram[...] = jnp.zeros_like(gram)

    flat = tensor_ref.reshape(sensors * slab_steps, chans)
    model = jnp.dot(chan_lhs[...], ct_ref[...], preferred_element_type=f32)
    lower_half = lax.broadcasted_iota(jnp.int32, (chans, 2 * rank), 1) < rank
    for pair in range(slab_steps // 2):
        wide, narrow = [], []
        for k in (2 * pair, 2 * pair + 1):
            piece = model[:, k * 2 * rank : (k + 1) * 2 * rank]
            top = piece.astype(bf16).astype(f32)
            wide.append(jnp.where(lower_half, top, piece - top).astype(bf16))
            narrow.append(jnp.where(lower_half, top, 0.0).astype(bf16))
        both = jnp.concatenate(wide, axis=0)
        first = jnp.concatenate(narrow, axis=0)
        data = jnp.concatenate(
            [flat[pl.ds(2 * pair, sensors, stride=slab_steps), :], flat[pl.ds(2 * pair + 1, sensors, stride=slab_steps), :]], axis=1
        )
        top, low = split(data)
        part = jnp.dot(fold_lhs[...], jnp.concatenate([top, low], axis=0), preferred_element_type=f32)
        own = lax.dot_general(
            square_lhs[...], jnp.concatenate([both, first], axis=1), (((1,), (1,)), ((), ())), preferred_element_type=f32
        )
        total = own - (part[:rank] + part[rank:])
        folded_ref[:, 2 * pair, :] = total[:, :chans]
        folded_ref[:, 2 * pair + 1, :] = total[:, chans:]
        fit_sum[...] += jnp.dot(
            jnp.concatenate([top, low], axis=1), jnp.concatenate([both, first], axis=0), preferred_element_type=f32
        )
        gram[...] += lax.dot_general(both, both, (((0,), (0,)), ((), ())), preferred_element_type=f32)

    @pl.when(step == steps - 1)
    def _():
        grams = gram[...]
        left = grams[:rank] + grams[rank:]
        square = left[:, :rank] + left[:, rank:]
        seen = fit_sum[...]
        model_fit = lax.dot_general(
            rows_ref[...], square, (((0,), (0,)), ((), ())), precision=highest, preferred_element_type=f32
        )
        fit_ref[...] = model_fit - (seen[:, :rank] + seen[:, rank:])


def big_pass(tensor, rows, chan, ct, slab_steps=8):
    sensors, times, chans = tensor.shape
    rank = rows.shape[0]
    rank_two = chan.shape[0]
    steps = times // slab_steps
    return pl.pallas_call(
        functools.partial(slab, steps),
        grid=(steps,),
        in_specs=[
            pl.BlockSpec((sensors, slab_steps, chans), lambda i: (0, i, 0)),
            pl.BlockSpec((rank, sensors), lambda i: (0, 0)),
            pl.BlockSpec((rank_two, chans), lambda i: (0, 0)),
            pl.BlockSpec((3 * rank_two, slab_steps * 2 * rank), lambda i: (0, i)),
        ],
        out_specs=[
            pl.BlockSpec((rank, slab_steps, chans), lambda i: (0, i, 0)),
            pl.BlockSpec((sensors, rank), lambda i: (0, 0)),
        ],
        out_shape=[jax.ShapeDtypeStruct((rank, times, chans), f32), jax.ShapeDtypeStruct((sensors, rank), f32)],
        scratch_shapes=[
            pltpu.VMEM((2 * rank, 2 * sensors), bf16),
            pltpu.VMEM((chans, 3 * rank_two), bf16),
            pltpu.VMEM((rank, 4 * rank), bf16),
            pltpu.VMEM((sensors, 2 * rank), f32),
            pltpu.VMEM((2 * rank, 2 * rank), f32),
        ],
        compiler_params=pltpu.CompilerParams(vmem_limit_bytes=50 * 2**20),
        cost_estimate=pl.CostEstimate(flops=8 * 10**9, bytes_accessed=32 * 2**20, transcendentals=0),
    )(tensor, rows, chan, ct)


def place():
    sensor = lax.axis_index("sensor")
    return lax.axis_index("channel"), sensor // 4, lax.axis_index("tm") * 2 + lax.rem(sensor // 2, 2), lax.rem(sensor, 2)


def device(x, y, z, core):
    return ((y * 2 + lax.rem(z, 2)) * 2 + core, x, z // 2)


def exchange(part_ref, fit_ref, total_ref, share_ref, half, from_core, from_x, quarter, from_y, piece, from_z, fit_x, fit_half, fit_z, sent, got):
    x, y, z, core = place()
    z_half = z // 2
    turn = lambda value, d: lax.rem(value + d, 4)
    x_peers = [(turn(x, d), y, z, core) for d in (1, 2, 3)]
    y_peers = [(x, turn(y, d), z, core) for d in (1, 2, 3)]
    z_peers = [(x, y, turn(z, d), core) for d in (1, 2, 3)]
    core_peer = (x, y, z, 1 - core)
    barrier = pltpu.get_barrier_semaphore()
    for peer in [core_peer] + x_peers + y_peers + z_peers:
        pl.semaphore_signal(barrier, inc=1, device_id=device(*peer), device_id_type=pl.DeviceIdType.MESH)
    pl.semaphore_wait(barrier, 10)

    slot = iter(range(21))

    def send(source, target, peer):
        at = next(slot)
        copy = pltpu.make_async_remote_copy(
            src_ref=source,
            dst_ref=target,
            send_sem=sent.at[at],
            recv_sem=got.at[at],
            device_id=device(*peer),
            device_id_type=pl.DeviceIdType.MESH,
        )
        copy.start()
        return copy

    to_core = send(part_ref.at[1 - core], from_core, core_peer)
    fits = [send(fit_ref.at[peer[0]], fit_x.at[d], peer) for d, peer in enumerate(x_peers)]
    to_core.wait()
    half[...] = part_ref[core] + from_core[...]
    over_x = [send(half.at[peer[0]], from_x.at[d], peer) for d, peer in enumerate(x_peers)]
    for copy in fits:
        copy.wait()
    fit_half[...] = (fit_ref[x] + fit_x[0]) + (fit_x[1] + fit_x[2])
    fit_last = send(fit_half.at[1 - z_half], fit_z, z_peers[1])
    for copy in over_x:
        copy.wait()
    quarter[...] = (half[x] + from_x[0]) + (from_x[1] + from_x[2])
    over_y = [send(quarter.at[peer[1]], from_y.at[d], peer) for d, peer in enumerate(y_peers)]
    fit_last.wait()
    share_ref[...] = fit_half[z_half] + fit_z[...]
    for copy in over_y:
        copy.wait()
    value = (quarter[y] + from_y[0]) + (from_y[1] + from_y[2])
    piece[...] = value
    from_z[z] = value
    over_z = [send(piece, from_z.at[z], peer) for peer in z_peers]
    for copy in over_z:
        copy.wait()
    piece[...] = (from_z[0] + from_z[1]) + (from_z[2] + from_z[3])
    total_ref[core, x, y] = piece[...]
    back_y = [send(piece, total_ref.at[core, x, y], peer) for peer in y_peers]
    for copy in back_y:
        copy.wait()
    back_x = [send(total_ref.at[core, x], total_ref.at[core, x], peer) for peer in x_peers]
    for copy in back_x:
        copy.wait()
    send(total_ref.at[core], total_ref.at[core], core_peer).wait()


def sum_all(part, fit):
    rows = part.shape[3]
    fit_rows = fit.shape[2]
    vmem = pl.BlockSpec(memory_space=pltpu.VMEM)
    return pl.pallas_call(
        exchange,
        in_specs=[vmem, vmem],
        out_specs=[vmem, vmem],
        out_shape=[jax.ShapeDtypeStruct(part.shape, f32), jax.ShapeDtypeStruct((fit_rows, 128), f32)],
        scratch_shapes=[
            pltpu.VMEM((4, 4, rows, 128), f32),
            pltpu.VMEM((4, 4, rows, 128), f32),
            pltpu.VMEM((3, 4, rows, 128), f32),
            pltpu.VMEM((4, rows, 128), f32),
            pltpu.VMEM((3, rows, 128), f32),
            pltpu.VMEM((rows, 128), f32),
            pltpu.VMEM((4, rows, 128), f32),
            pltpu.VMEM((3, 2, fit_rows, 128), f32),
            pltpu.VMEM((2, fit_rows, 128), f32),
            pltpu.VMEM((fit_rows, 128), f32),
            pltpu.SemaphoreType.DMA((21,)),
            pltpu.SemaphoreType.DMA((21,)),
        ],
        compiler_params=pltpu.CompilerParams(collective_id=0, has_side_effects=True),
    )(part, fit)


def on_device(
    tensor, core, sensor_factor, channel_factor, time_factor, neighbour_ids, edge_weights
):
    sensor_rows, time_rows, chan_rows = tensor.shape
    rank_one, rank_two, rank_three = core.shape
    n_sensor = lax.axis_size("sensor")
    n_channel = lax.axis_size("channel")
    n_time = lax.axis_size("tm")
    total_sensors = sensor_rows * n_sensor
    total_time = time_rows * n_time
    total_chan = chan_rows * n_channel
    groups = n_channel * n_time
    chan_index = lax.axis_index("channel")
    time_index = lax.axis_index("tm")
    share_index = chan_index * n_time + time_index
    share = sensor_rows // groups
    block, slots = edge_weights.shape[-1], edge_weights.shape[1]
    blocks = edge_weights.shape[0]

    rows = sensor_factor.T
    block_rows = rows.reshape(rank_one, blocks, block).transpose(1, 0, 2)
    whole_rows = lax.all_gather(block_rows, "sensor", axis=0, tiled=True)

    core_time = jnp.einsum("rst,kt->skr", core, time_factor, precision=highest)
    twice = jnp.concatenate([core_time, core_time], axis=2).reshape(rank_two, time_rows * 2 * rank_one)
    top = lax.reduce_precision(twice, 8, 7)
    ct = jnp.concatenate([top, top, twice - top], axis=0).astype(bf16)
    folded3, fit = big_pass(tensor, rows, channel_factor.T, ct)

    pairs = blocks * slots // groups
    first = share_index * pairs
    weights = lax.dynamic_slice_in_dim(edge_weights.reshape(blocks * slots, block, block), first, pairs, 0).astype(f32)
    ids = lax.dynamic_slice_in_dim(neighbour_ids.reshape(blocks * slots), first, pairs, 0)
    near = jnp.stack([lax.dynamic_index_in_dim(whole_rows, ids[q], 0, keepdims=False) for q in range(pairs)])
    pulled = jnp.einsum("qac,qdc->qad", weights, near, precision=high)
    degree = jnp.sum(weights, axis=2)
    owner = (first + jnp.arange(pairs)) // slots
    chosen = (jnp.arange(blocks)[:, None] == owner[None, :]).astype(f32)
    degrees = jnp.sum(chosen[:, :, None] * degree[None], axis=1).reshape(sensor_rows)
    pulls = jnp.sum(chosen[:, :, None, None] * pulled[None], axis=1).reshape(sensor_rows, rank_one)
    fit_part = fit / math.sqrt(total_time * total_chan) + lap_weight * (degrees[:, None] * sensor_factor - pulls)
    fit_pack = fit_part.reshape(n_channel, n_time, 2, share // 2, rank_one)
    fit_pack = jnp.concatenate([fit_pack[:, :, 0], fit_pack[:, :, 1]], axis=-1)

    inner = jnp.einsum("rkj,js->rks", folded3, channel_factor, precision=high)
    core_part = jnp.einsum("rks,kt->rts", inner, time_factor, precision=high)
    chan_part = jnp.einsum("rkj,skr->sj", folded3, core_time, precision=high)
    time_part = jnp.einsum("rks,rst->tk", inner, core, precision=high)
    chan_slots = jnp.where((jnp.arange(n_channel) == chan_index)[:, None, None], chan_part[None], 0.0)
    time_slots = jnp.where((jnp.arange(n_time) == time_index)[:, None, None], time_part[None], 0.0)
    n_core = core_part.size // 128
    n_chan = n_channel * chan_part.size // 128
    n_rows = n_core + n_chan + n_time * time_part.size // 128
    piece_rows = -(-n_rows // 256) * 8
    packed = jnp.concatenate(
        [
            (core_part / math.sqrt(total_sensors * total_time * total_chan)).reshape(-1, 128),
            (chan_slots / math.sqrt(total_sensors * total_time)).reshape(-1, 128),
            (time_slots / math.sqrt(total_sensors * total_chan)).reshape(-1, 128),
            jnp.zeros((32 * piece_rows - n_rows, 128), f32),
        ],
        axis=0,
    ).reshape(2, 4, 4, piece_rows, 128)
    total, fit_share = sum_all(packed, fit_pack)
    sensor_grad = jnp.concatenate([fit_share[:, :rank_one], fit_share[:, rank_one:]], axis=0)
    total = total.reshape(-1, 128)
    core_grad = total[:n_core].reshape(rank_one, rank_three, rank_two).transpose(0, 2, 1)
    chan_all = total[n_core : n_core + n_chan].reshape(n_channel, rank_two, chan_rows)
    time_all = total[n_core + n_chan : n_rows].reshape(n_time, rank_three, time_rows)
    channel_grad = lax.dynamic_index_in_dim(chan_all, chan_index, 0, keepdims=False).T
    time_grad = lax.dynamic_index_in_dim(time_all, time_index, 0, keepdims=False).T
    return (core_grad, sensor_grad, channel_grad, time_grad)


def solution(mesh):
    return jax.shard_map(
        on_device,
        mesh=mesh,
        in_specs=(
            P("sensor", "tm", "channel"),
            P(),
            P("sensor", None),
            P("channel", None),
            P("tm", None),
            P("sensor", None),
            P("sensor", None, None, None),
        ),
        out_specs=(P(), P(("sensor", "channel", "tm"), None), P("channel", None), P("tm", None)),
        check_vma=False,
    )
```

```python
import functools
import math

import jax
import jax.numpy as jnp
from jax import lax
from jax.experimental import pallas as pl
from jax.experimental.pallas import tpu as pltpu
from jax.sharding import PartitionSpec as P

lap_weight = 1.0 / 512.0
high = lax.Precision.HIGH
highest = lax.Precision.HIGHEST
f32 = jnp.float32
bf16 = jnp.bfloat16


def split(value):
    top = value.astype(bf16)
    return top, (value - top.astype(f32)).astype(bf16)


def slab(steps, tensor_ref, rows_ref, chan_ref, ct_ref, inner_ref, by_chan_ref, fit_ref, fold_lhs, chan_lhs, chan_rhs, square_lhs, fit_sum, gram, by_chan):
    step = pl.program_id(0)
    sensors, slab_steps, chans = tensor_ref.shape
    rank = rows_ref.shape[0]

    @pl.when(step == 0)
    def _():
        rows = rows_ref[...]
        top, low = split(rows)
        fold_lhs[0:rank, 0:sensors] = top
        fold_lhs[0:rank, sensors:] = top
        fold_lhs[rank:, 0:sensors] = low
        fold_lhs[rank:, sensors:] = jnp.zeros_like(low)
        square = lax.dot_general(rows, rows, (((1,), (1,)), ((), ())), precision=highest, preferred_element_type=f32)
        top, low = split(square)
        square_lhs[...] = jnp.concatenate([top, top, low, jnp.zeros_like(low)], axis=1)
        top, low = split(chan_ref[...].T)
        chan_lhs[...] = jnp.concatenate([top, low, top], axis=1)
        chan_rhs[...] = jnp.concatenate(
            [jnp.concatenate([top, low], axis=1), jnp.concatenate([top, jnp.zeros_like(low)], axis=1)], axis=0
        )
        by_chan[...] = jnp.zeros_like(by_chan)
        fit_sum[...] = jnp.zeros_like(fit_sum)
        gram[...] = jnp.zeros_like(gram)

    flat = tensor_ref.reshape(sensors * slab_steps, chans)
    ct_top, ct_low = split(ct_ref[...])
    model = jnp.dot(chan_lhs[...], jnp.concatenate([ct_top, ct_top, ct_low], axis=0), preferred_element_type=f32)
    stacked, across = [], []
    lower_half = lax.broadcasted_iota(jnp.int32, (chans, 2 * rank), 1) < rank
    for pair in range(slab_steps // 2):
        wide, narrow = [], []
        for k in (2 * pair, 2 * pair + 1):
            piece = model[:, k * 2 * rank : (k + 1) * 2 * rank]
            top = piece.astype(bf16).astype(f32)
            wide.append(jnp.where(lower_half, top, piece - top).astype(bf16))
            narrow.append(jnp.where(lower_half, top, 0.0).astype(bf16))
        both = jnp.concatenate(wide, axis=0)
        first = jnp.concatenate(narrow, axis=0)
        data = jnp.concatenate(
            [flat[pl.ds(2 * pair, sensors, stride=slab_steps), :], flat[pl.ds(2 * pair + 1, sensors, stride=slab_steps), :]], axis=1
        )
        top, low = split(data)
        part = jnp.dot(fold_lhs[...], jnp.concatenate([top, low], axis=0), preferred_element_type=f32)
        own = lax.dot_general(
            square_lhs[...], jnp.concatenate([both, first], axis=1), (((1,), (1,)), ((), ())), preferred_element_type=f32
        )
        total = own - (part[:rank] + part[rank:])
        total_top, total_low = split(total)
        for k in (0, 1):
            cut = slice(k * chans, (k + 1) * chans)
            stacked += [total_top[:, cut], total_low[:, cut]]
            across.append(jnp.concatenate([total_top[:, cut], total_low[:, cut]], axis=1))
        fit_sum[...] += jnp.dot(
            jnp.concatenate([top, low], axis=1), jnp.concatenate([both, first], axis=0), preferred_element_type=f32
        )
        gram[...] += lax.dot_general(both, both, (((0,), (0,)), ((), ())), preferred_element_type=f32)

    by_chan[...] += jnp.dot(
        jnp.concatenate([ct_top, ct_low], axis=0), jnp.concatenate(stacked, axis=0), preferred_element_type=f32
    )
    inner = jnp.dot(jnp.concatenate(across, axis=0), chan_rhs[...], preferred_element_type=f32)
    rank_two = inner.shape[1] // 2
    inner = inner[:, :rank_two] + inner[:, rank_two:]
    for k in range(slab_steps):
        upper = inner[k * rank : k * rank + rank // 2]
        inner_ref[k] = jnp.concatenate([upper, inner[k * rank + rank // 2 : (k + 1) * rank]], axis=1)

    @pl.when(step == steps - 1)
    def _():
        chan_sums = by_chan[...]
        by_chan_ref[...] = chan_sums[:rank_two] + chan_sums[rank_two:]
        grams = gram[...]
        left = grams[:rank] + grams[rank:]
        square = left[:, :rank] + left[:, rank:]
        seen = fit_sum[...]
        model_fit = lax.dot_general(
            rows_ref[...], square, (((0,), (0,)), ((), ())), precision=highest, preferred_element_type=f32
        )
        fit_ref[...] = model_fit - (seen[:, :rank] + seen[:, rank:])


def big_pass(tensor, rows, chan, ct, slab_steps=8):
    sensors, times, chans = tensor.shape
    rank = rows.shape[0]
    rank_two = chan.shape[0]
    steps = times // slab_steps
    return pl.pallas_call(
        functools.partial(slab, steps),
        grid=(steps,),
        in_specs=[
            pl.BlockSpec((sensors, slab_steps, chans), lambda i: (0, i, 0)),
            pl.BlockSpec((rank, sensors), lambda i: (0, 0)),
            pl.BlockSpec((rank_two, chans), lambda i: (0, 0)),
            pl.BlockSpec((rank_two, slab_steps * 2 * rank), lambda i: (0, i)),
        ],
        out_specs=[
            pl.BlockSpec((slab_steps, rank // 2, 2 * rank_two), lambda i: (i, 0, 0)),
            pl.BlockSpec((rank_two, chans), lambda i: (0, 0)),
            pl.BlockSpec((sensors, rank), lambda i: (0, 0)),
        ],
        out_shape=[
            jax.ShapeDtypeStruct((times, rank // 2, 2 * rank_two), f32),
            jax.ShapeDtypeStruct((rank_two, chans), f32),
            jax.ShapeDtypeStruct((sensors, rank), f32),
        ],
        scratch_shapes=[
            pltpu.VMEM((2 * rank, 2 * sensors), bf16),
            pltpu.VMEM((chans, 3 * rank_two), bf16),
            pltpu.VMEM((2 * chans, 2 * rank_two), bf16),
            pltpu.VMEM((rank, 4 * rank), bf16),
            pltpu.VMEM((sensors, 2 * rank), f32),
            pltpu.VMEM((2 * rank, 2 * rank), f32),
            pltpu.VMEM((2 * rank_two, chans), f32),
        ],
        compiler_params=pltpu.CompilerParams(vmem_limit_bytes=50 * 2**20),
        cost_estimate=pl.CostEstimate(flops=8 * 10**9, bytes_accessed=32 * 2**20, transcendentals=0),
    )(tensor, rows, chan, ct)


def place():
    sensor = lax.axis_index("sensor")
    return lax.axis_index("channel"), sensor // 4, lax.axis_index("tm") * 2 + lax.rem(sensor // 2, 2), lax.rem(sensor, 2)


def device(x, y, z, core):
    return ((y * 2 + lax.rem(z, 2)) * 2 + core, x, z // 2)


def exchange(part_ref, fit_ref, total_ref, share_ref, half, from_core, from_x, quarter, from_y, piece, from_z, fit_x, fit_half, fit_z, sent, got):
    x, y, z, core = place()
    z_half = z // 2
    turn = lambda value, d: lax.rem(value + d, 4)
    x_peers = [(turn(x, d), y, z, core) for d in (1, 2, 3)]
    y_peers = [(x, turn(y, d), z, core) for d in (1, 2, 3)]
    z_peers = [(x, y, turn(z, d), core) for d in (1, 2, 3)]
    core_peer = (x, y, z, 1 - core)
    barrier = pltpu.get_barrier_semaphore()
    for peer in [core_peer] + x_peers + y_peers + z_peers:
        pl.semaphore_signal(barrier, inc=1, device_id=device(*peer), device_id_type=pl.DeviceIdType.MESH)
    pl.semaphore_wait(barrier, 10)

    slot = iter(range(21))

    def send(source, target, peer):
        at = next(slot)
        copy = pltpu.make_async_remote_copy(
            src_ref=source,
            dst_ref=target,
            send_sem=sent.at[at],
            recv_sem=got.at[at],
            device_id=device(*peer),
            device_id_type=pl.DeviceIdType.MESH,
        )
        copy.start()
        return copy

    to_core = send(part_ref.at[1 - core], from_core, core_peer)
    fits = [send(fit_ref.at[peer[0]], fit_x.at[d], peer) for d, peer in enumerate(x_peers)]
    to_core.wait()
    half[...] = part_ref[core] + from_core[...]
    over_x = [send(half.at[peer[0]], from_x.at[d], peer) for d, peer in enumerate(x_peers)]
    for copy in fits:
        copy.wait()
    fit_half[...] = (fit_ref[x] + fit_x[0]) + (fit_x[1] + fit_x[2])
    fit_last = send(fit_half.at[1 - z_half], fit_z, z_peers[1])
    for copy in over_x:
        copy.wait()
    quarter[...] = (half[x] + from_x[0]) + (from_x[1] + from_x[2])
    over_y = [send(quarter.at[peer[1]], from_y.at[d], peer) for d, peer in enumerate(y_peers)]
    fit_last.wait()
    share_ref[...] = fit_half[z_half] + fit_z[...]
    for copy in over_y:
        copy.wait()
    value = (quarter[y] + from_y[0]) + (from_y[1] + from_y[2])
    piece[...] = value
    from_z[z] = value
    over_z = [send(piece, from_z.at[z], peer) for peer in z_peers]
    for copy in over_z:
        copy.wait()
    piece[...] = (from_z[0] + from_z[1]) + (from_z[2] + from_z[3])
    total_ref[core, x, y] = piece[...]
    back_y = [send(piece, total_ref.at[core, x, y], peer) for peer in y_peers]
    for copy in back_y:
        copy.wait()
    back_x = [send(total_ref.at[core, x], total_ref.at[core, x], peer) for peer in x_peers]
    for copy in back_x:
        copy.wait()
    send(total_ref.at[core], total_ref.at[core], core_peer).wait()


def sum_all(part, fit):
    rows = part.shape[3]
    fit_rows = fit.shape[2]
    vmem = pl.BlockSpec(memory_space=pltpu.VMEM)
    return pl.pallas_call(
        exchange,
        in_specs=[vmem, vmem],
        out_specs=[vmem, vmem],
        out_shape=[jax.ShapeDtypeStruct(part.shape, f32), jax.ShapeDtypeStruct((fit_rows, 128), f32)],
        scratch_shapes=[
            pltpu.VMEM((4, 4, rows, 128), f32),
            pltpu.VMEM((4, 4, rows, 128), f32),
            pltpu.VMEM((3, 4, rows, 128), f32),
            pltpu.VMEM((4, rows, 128), f32),
            pltpu.VMEM((3, rows, 128), f32),
            pltpu.VMEM((rows, 128), f32),
            pltpu.VMEM((4, rows, 128), f32),
            pltpu.VMEM((3, 2, fit_rows, 128), f32),
            pltpu.VMEM((2, fit_rows, 128), f32),
            pltpu.VMEM((fit_rows, 128), f32),
            pltpu.SemaphoreType.DMA((21,)),
            pltpu.SemaphoreType.DMA((21,)),
        ],
        compiler_params=pltpu.CompilerParams(collective_id=0, has_side_effects=True),
    )(part, fit)


def on_device(
    tensor, core, sensor_factor, channel_factor, time_factor, neighbour_ids, edge_weights
):
    sensor_rows, time_rows, chan_rows = tensor.shape
    rank_one, rank_two, rank_three = core.shape
    n_sensor = lax.axis_size("sensor")
    n_channel = lax.axis_size("channel")
    n_time = lax.axis_size("tm")
    total_sensors = sensor_rows * n_sensor
    total_time = time_rows * n_time
    total_chan = chan_rows * n_channel
    groups = n_channel * n_time
    chan_index = lax.axis_index("channel")
    time_index = lax.axis_index("tm")
    share_index = chan_index * n_time + time_index
    share = sensor_rows // groups
    block, slots = edge_weights.shape[-1], edge_weights.shape[1]
    blocks = edge_weights.shape[0]

    rows = sensor_factor.T
    block_rows = rows.reshape(rank_one, blocks, block).transpose(1, 0, 2)
    whole_rows = lax.all_gather(block_rows, "sensor", axis=0, tiled=True)

    by_rank = core.transpose(1, 2, 0)
    twice = jnp.einsum("kt,str->skr", time_factor, jnp.concatenate([by_rank, by_rank], axis=2), precision=highest)
    inner, chan_part, fit = big_pass(
        tensor, rows, channel_factor.T, twice.reshape(rank_two, time_rows * 2 * rank_one)
    )

    pairs = blocks * slots // groups
    first = share_index * pairs
    weights = lax.dynamic_slice_in_dim(edge_weights.reshape(blocks * slots, block, block), first, pairs, 0).astype(f32)
    ids = lax.dynamic_slice_in_dim(neighbour_ids.reshape(blocks * slots), first, pairs, 0)
    near = jnp.stack([lax.dynamic_index_in_dim(whole_rows, ids[q], 0, keepdims=False) for q in range(pairs)])
    pulled = jnp.einsum("qac,qdc->qad", weights, near, precision=high)
    degree = jnp.sum(weights, axis=2)
    owner = (first + jnp.arange(pairs)) // slots
    chosen = (jnp.arange(blocks)[:, None] == owner[None, :]).astype(f32)
    degrees = jnp.sum(chosen[:, :, None] * degree[None], axis=1).reshape(sensor_rows)
    pulls = jnp.sum(chosen[:, :, None, None] * pulled[None], axis=1).reshape(sensor_rows, rank_one)
    fit_part = fit / math.sqrt(total_time * total_chan) + lap_weight * (degrees[:, None] * sensor_factor - pulls)
    fit_pack = fit_part.reshape(n_channel, n_time, 2, share // 2, rank_one)
    fit_pack = jnp.concatenate([fit_pack[:, :, 0], fit_pack[:, :, 1]], axis=-1)

    halves = core.reshape(2, rank_one // 2, rank_two, rank_three).transpose(3, 1, 0, 2).reshape(rank_three, rank_one // 2, 2 * rank_two)
    core_part = jnp.einsum("kt,kam->tam", time_factor, inner, precision=high)
    time_part = jnp.einsum("kam,tam->tk", inner, halves, precision=high)
    chan_slots = jnp.where((jnp.arange(n_channel) == chan_index)[:, None, None], chan_part[None], 0.0)
    time_slots = jnp.where((jnp.arange(n_time) == time_index)[:, None, None], time_part[None], 0.0)
    n_core = core_part.size // 128
    n_chan = n_channel * chan_part.size // 128
    n_rows = n_core + n_chan + n_time * time_part.size // 128
    piece_rows = -(-n_rows // 256) * 8
    packed = jnp.concatenate(
        [
            (core_part / math.sqrt(total_sensors * total_time * total_chan)).reshape(-1, 128),
            (chan_slots / math.sqrt(total_sensors * total_time)).reshape(-1, 128),
            (time_slots / math.sqrt(total_sensors * total_chan)).reshape(-1, 128),
            jnp.zeros((32 * piece_rows - n_rows, 128), f32),
        ],
        axis=0,
    ).reshape(2, 4, 4, piece_rows, 128)
    total, fit_share = sum_all(packed, fit_pack)
    sensor_grad = jnp.concatenate([fit_share[:, :rank_one], fit_share[:, rank_one:]], axis=0)
    total = total.reshape(-1, 128)
    core_sum = total[:n_core].reshape(rank_three, rank_one // 2, 2, rank_two)
    core_grad = core_sum.transpose(2, 1, 3, 0).reshape(rank_one, rank_two, rank_three)
    chan_all = total[n_core : n_core + n_chan].reshape(n_channel, rank_two, chan_rows)
    time_all = total[n_core + n_chan : n_rows].reshape(n_time, rank_three, time_rows)
    channel_grad = lax.dynamic_index_in_dim(chan_all, chan_index, 0, keepdims=False).T
    time_grad = lax.dynamic_index_in_dim(time_all, time_index, 0, keepdims=False).T
    return (core_grad, sensor_grad, channel_grad, time_grad)


def solution(mesh):
    return jax.shard_map(
        on_device,
        mesh=mesh,
        in_specs=(
            P("sensor", "tm", "channel"),
            P(),
            P("sensor", None),
            P("channel", None),
            P("tm", None),
            P("sensor", None),
            P("sensor", None, None, None),
        ),
        out_specs=(P(), P(("sensor", "channel", "tm"), None), P("channel", None), P("tm", None)),
        check_vma=False,
    )
```

```python
import functools
import math

import jax
import jax.numpy as jnp
from jax import lax
from jax.experimental import pallas as pl
from jax.experimental.pallas import tpu as pltpu
from jax.sharding import PartitionSpec as P

lap_weight = 1.0 / 512.0
high = lax.Precision.HIGH
highest = lax.Precision.HIGHEST
f32 = jnp.float32
bf16 = jnp.bfloat16


def split(value):
    top = value.astype(bf16)
    return top, (value - top.astype(f32)).astype(bf16)


def slab(steps, tensor_ref, rows_ref, chan_ref, ct_ref, inner_ref, by_chan_ref, fit_ref, fold_lhs, chan_lhs, chan_rhs, square_lhs, fit_sum, gram, by_chan):
    step = pl.program_id(0)
    sensors, slab_steps, chans = tensor_ref.shape
    rank = rows_ref.shape[0]

    @pl.when(step == 0)
    def _():
        rows = rows_ref[...]
        top, low = split(rows)
        fold_lhs[0:rank, 0:sensors] = top
        fold_lhs[0:rank, sensors:] = top
        fold_lhs[rank:, 0:sensors] = low
        fold_lhs[rank:, sensors:] = jnp.zeros_like(low)
        square = lax.dot_general(rows, rows, (((1,), (1,)), ((), ())), precision=highest, preferred_element_type=f32)
        top, low = split(square)
        square_lhs[...] = jnp.concatenate([top, top, low, jnp.zeros_like(low)], axis=1)
        top, low = split(chan_ref[...].T)
        chan_lhs[...] = jnp.concatenate([top, low, top], axis=1)
        chan_rhs[...] = jnp.concatenate(
            [jnp.concatenate([top, low], axis=1), jnp.concatenate([top, jnp.zeros_like(low)], axis=1)], axis=0
        )
        by_chan[...] = jnp.zeros_like(by_chan)
        fit_sum[...] = jnp.zeros_like(fit_sum)
        gram[...] = jnp.zeros_like(gram)

    flat = tensor_ref.reshape(sensors * slab_steps, chans)
    ct_top, ct_low = split(ct_ref[...])
    model = jnp.dot(chan_lhs[...], jnp.concatenate([ct_top, ct_top, ct_low], axis=0), preferred_element_type=f32)
    stacked, across = [], []
    lower_half = lax.broadcasted_iota(jnp.int32, (chans, 2 * rank), 1) < rank
    for pair in range(slab_steps // 2):
        wide, narrow = [], []
        for k in (2 * pair, 2 * pair + 1):
            piece = model[:, k * 2 * rank : (k + 1) * 2 * rank]
            top = piece.astype(bf16).astype(f32)
            wide.append(jnp.where(lower_half, top, piece - top).astype(bf16))
            narrow.append(jnp.where(lower_half, top, 0.0).astype(bf16))
        both = jnp.concatenate(wide, axis=0)
        first = jnp.concatenate(narrow, axis=0)
        data = jnp.concatenate(
            [flat[pl.ds(2 * pair, sensors, stride=slab_steps), :], flat[pl.ds(2 * pair + 1, sensors, stride=slab_steps), :]], axis=1
        )
        top, low = split(data)
        part = jnp.dot(fold_lhs[...], jnp.concatenate([top, low], axis=0), preferred_element_type=f32)
        own = lax.dot_general(
            square_lhs[...], jnp.concatenate([both, first], axis=1), (((1,), (1,)), ((), ())), preferred_element_type=f32
        )
        total = own - (part[:rank] + part[rank:])
        total_top, total_low = split(total)
        for k in (0, 1):
            cut = slice(k * chans, (k + 1) * chans)
            stacked += [total_top[:, cut], total_low[:, cut]]
            across.append(jnp.concatenate([total_top[:, cut], total_low[:, cut]], axis=1))
        fit_sum[...] += jnp.dot(
            jnp.concatenate([top, low], axis=1), jnp.concatenate([both, first], axis=0), preferred_element_type=f32
        )
        gram[...] += lax.dot_general(both, both, (((0,), (0,)), ((), ())), preferred_element_type=f32)

    by_chan[...] += jnp.dot(
        jnp.concatenate([ct_top, ct_low], axis=0), jnp.concatenate(stacked, axis=0), preferred_element_type=f32
    )
    inner = jnp.dot(jnp.concatenate(across, axis=0), chan_rhs[...], preferred_element_type=f32)
    rank_two = inner.shape[1] // 2
    inner = inner[:, :rank_two] + inner[:, rank_two:]
    for k in range(slab_steps):
        upper = inner[k * rank : k * rank + rank // 2]
        inner_ref[k] = jnp.concatenate([upper, inner[k * rank + rank // 2 : (k + 1) * rank]], axis=1)

    @pl.when(step == steps - 1)
    def _():
        chan_sums = by_chan[...]
        by_chan_ref[...] = chan_sums[:rank_two] + chan_sums[rank_two:]
        grams = gram[...]
        left = grams[:rank] + grams[rank:]
        square = left[:, :rank] + left[:, rank:]
        seen = fit_sum[...]
        model_fit = lax.dot_general(
            rows_ref[...], square, (((0,), (0,)), ((), ())), precision=highest, preferred_element_type=f32
        )
        fit_ref[...] = model_fit - (seen[:, :rank] + seen[:, rank:])


def big_pass(tensor, rows, chan, ct, slab_steps=8):
    sensors, times, chans = tensor.shape
    rank = rows.shape[0]
    rank_two = chan.shape[0]
    steps = times // slab_steps
    return pl.pallas_call(
        functools.partial(slab, steps),
        grid=(steps,),
        in_specs=[
            pl.BlockSpec((sensors, slab_steps, chans), lambda i: (0, i, 0)),
            pl.BlockSpec((rank, sensors), lambda i: (0, 0)),
            pl.BlockSpec((rank_two, chans), lambda i: (0, 0)),
            pl.BlockSpec((rank_two, slab_steps * 2 * rank), lambda i: (0, i)),
        ],
        out_specs=[
            pl.BlockSpec((slab_steps, rank // 2, 2 * rank_two), lambda i: (i, 0, 0)),
            pl.BlockSpec((rank_two, chans), lambda i: (0, 0)),
            pl.BlockSpec((sensors, rank), lambda i: (0, 0)),
        ],
        out_shape=[
            jax.ShapeDtypeStruct((times, rank // 2, 2 * rank_two), f32),
            jax.ShapeDtypeStruct((rank_two, chans), f32),
            jax.ShapeDtypeStruct((sensors, rank), f32),
        ],
        scratch_shapes=[
            pltpu.VMEM((2 * rank, 2 * sensors), bf16),
            pltpu.VMEM((chans, 3 * rank_two), bf16),
            pltpu.VMEM((2 * chans, 2 * rank_two), bf16),
            pltpu.VMEM((rank, 4 * rank), bf16),
            pltpu.VMEM((sensors, 2 * rank), f32),
            pltpu.VMEM((2 * rank, 2 * rank), f32),
            pltpu.VMEM((2 * rank_two, chans), f32),
        ],
        compiler_params=pltpu.CompilerParams(vmem_limit_bytes=50 * 2**20),
        cost_estimate=pl.CostEstimate(flops=8 * 10**9, bytes_accessed=32 * 2**20, transcendentals=0),
    )(tensor, rows, chan, ct)


def place():
    sensor = lax.axis_index("sensor")
    return lax.axis_index("channel"), sensor // 4, lax.axis_index("tm") * 2 + lax.rem(sensor // 2, 2), lax.rem(sensor, 2)


def device(x, y, z, core):
    return ((y * 2 + lax.rem(z, 2)) * 2 + core, x, z // 2)


def exchange(part_ref, fit_ref, total_ref, share_ref, half, from_core, from_x, quarter, from_y, piece, from_z, fit_x, fit_half, fit_z, sent, got):
    x, y, z, core = place()
    z_half = z // 2
    turn = lambda value, d: lax.rem(value + d, 4)
    x_peers = [(turn(x, d), y, z, core) for d in (1, 2, 3)]
    y_peers = [(x, turn(y, d), z, core) for d in (1, 2, 3)]
    z_peers = [(x, y, turn(z, d), core) for d in (1, 2, 3)]
    core_peer = (x, y, z, 1 - core)
    barrier = pltpu.get_barrier_semaphore()
    for peer in [core_peer] + x_peers + y_peers + z_peers:
        pl.semaphore_signal(barrier, inc=1, device_id=device(*peer), device_id_type=pl.DeviceIdType.MESH)
    pl.semaphore_wait(barrier, 10)

    slot = iter(range(27))

    def send(source, target, peer):
        at = next(slot)
        copy = pltpu.make_async_remote_copy(
            src_ref=source,
            dst_ref=target,
            send_sem=sent.at[at],
            recv_sem=got.at[at],
            device_id=device(*peer),
            device_id_type=pl.DeviceIdType.MESH,
        )
        copy.start()
        return copy

    order = [peer[0] for peer in x_peers] + [x]
    to_core = [send(part_ref.at[1 - core, at], from_core.at[at], core_peer) for at in order]
    fits = [send(fit_ref.at[peer[0]], fit_x.at[d], peer) for d, peer in enumerate(x_peers)]
    over_x = []
    for d, at in enumerate(order):
        to_core[d].wait()
        half[at] = part_ref[core, at] + from_core[at]
        if d < 3:
            over_x.append(send(half.at[at], from_x.at[d], x_peers[d]))
    for copy in fits:
        copy.wait()
    fit_half[...] = (fit_ref[x] + fit_x[0]) + (fit_x[1] + fit_x[2])
    fit_last = send(fit_half.at[1 - z_half], fit_z, z_peers[1])
    for copy in over_x:
        copy.wait()
    quarter[...] = (half[x] + from_x[0]) + (from_x[1] + from_x[2])
    over_y = [send(quarter.at[peer[1]], from_y.at[d], peer) for d, peer in enumerate(y_peers)]
    fit_last.wait()
    share_ref[...] = fit_half[z_half] + fit_z[...]
    for copy in over_y:
        copy.wait()
    value = (quarter[y] + from_y[0]) + (from_y[1] + from_y[2])
    piece[...] = value
    from_z[z] = value
    over_z = [send(piece, from_z.at[z], peer) for peer in z_peers]
    for copy in over_z:
        copy.wait()
    piece[...] = (from_z[0] + from_z[1]) + (from_z[2] + from_z[3])
    total_ref[core, x, y] = piece[...]
    back_y = [send(piece, total_ref.at[core, x, y], peer) for peer in y_peers]
    for copy in back_y:
        copy.wait()
    back_x = [send(total_ref.at[core, x], total_ref.at[core, x], peer) for peer in x_peers]
    across = [send(total_ref.at[core, x], total_ref.at[core, x], core_peer)]
    for d, copy in enumerate(back_x):
        copy.wait()
        came = turn(x, 3 - d)
        across.append(send(total_ref.at[core, came], total_ref.at[core, came], core_peer))
    for copy in across:
        copy.wait()


def sum_all(part, fit):
    rows = part.shape[3]
    fit_rows = fit.shape[2]
    vmem = pl.BlockSpec(memory_space=pltpu.VMEM)
    return pl.pallas_call(
        exchange,
        in_specs=[vmem, vmem],
        out_specs=[vmem, vmem],
        out_shape=[jax.ShapeDtypeStruct(part.shape, f32), jax.ShapeDtypeStruct((fit_rows, 128), f32)],
        scratch_shapes=[
            pltpu.VMEM((4, 4, rows, 128), f32),
            pltpu.VMEM((4, 4, rows, 128), f32),
            pltpu.VMEM((3, 4, rows, 128), f32),
            pltpu.VMEM((4, rows, 128), f32),
            pltpu.VMEM((3, rows, 128), f32),
            pltpu.VMEM((rows, 128), f32),
            pltpu.VMEM((4, rows, 128), f32),
            pltpu.VMEM((3, 2, fit_rows, 128), f32),
            pltpu.VMEM((2, fit_rows, 128), f32),
            pltpu.VMEM((fit_rows, 128), f32),
            pltpu.SemaphoreType.DMA((27,)),
            pltpu.SemaphoreType.DMA((27,)),
        ],
        compiler_params=pltpu.CompilerParams(collective_id=0, has_side_effects=True),
    )(part, fit)


def on_device(
    tensor, core, sensor_factor, channel_factor, time_factor, neighbour_ids, edge_weights
):
    sensor_rows, time_rows, chan_rows = tensor.shape
    rank_one, rank_two, rank_three = core.shape
    n_sensor = lax.axis_size("sensor")
    n_channel = lax.axis_size("channel")
    n_time = lax.axis_size("tm")
    total_sensors = sensor_rows * n_sensor
    total_time = time_rows * n_time
    total_chan = chan_rows * n_channel
    groups = n_channel * n_time
    chan_index = lax.axis_index("channel")
    time_index = lax.axis_index("tm")
    share_index = chan_index * n_time + time_index
    share = sensor_rows // groups
    block, slots = edge_weights.shape[-1], edge_weights.shape[1]
    blocks = edge_weights.shape[0]

    rows = sensor_factor.T
    block_rows = rows.reshape(rank_one, blocks, block).transpose(1, 0, 2)
    whole_rows = lax.all_gather(block_rows, "sensor", axis=0, tiled=True)

    by_rank = core.transpose(1, 2, 0)
    twice = jnp.einsum("kt,str->skr", time_factor, jnp.concatenate([by_rank, by_rank], axis=2), precision=highest)
    inner, chan_part, fit = big_pass(
        tensor, rows, channel_factor.T, twice.reshape(rank_two, time_rows * 2 * rank_one)
    )

    pairs = blocks * slots // groups
    first = share_index * pairs
    weights = lax.dynamic_slice_in_dim(edge_weights.reshape(blocks * slots, block, block), first, pairs, 0).astype(f32)
    ids = lax.dynamic_slice_in_dim(neighbour_ids.reshape(blocks * slots), first, pairs, 0)
    near = jnp.stack([lax.dynamic_index_in_dim(whole_rows, ids[q], 0, keepdims=False) for q in range(pairs)])
    pulled = jnp.einsum("qac,qdc->qad", weights, near, precision=high)
    degree = jnp.sum(weights, axis=2)
    owner = (first + jnp.arange(pairs)) // slots
    chosen = (jnp.arange(blocks)[:, None] == owner[None, :]).astype(f32)
    degrees = jnp.sum(chosen[:, :, None] * degree[None], axis=1).reshape(sensor_rows)
    pulls = jnp.sum(chosen[:, :, None, None] * pulled[None], axis=1).reshape(sensor_rows, rank_one)
    fit_part = fit / math.sqrt(total_time * total_chan) + lap_weight * (degrees[:, None] * sensor_factor - pulls)
    fit_pack = fit_part.reshape(n_channel, n_time, 2, share // 2, rank_one)
    fit_pack = jnp.concatenate([fit_pack[:, :, 0], fit_pack[:, :, 1]], axis=-1)

    core_part = jnp.einsum("kt,kam->tam", time_factor, inner, precision=high)
    half = rank_one // 2
    time_part = jnp.einsum("kas,ast->tk", inner[:, :, :rank_two], core[:half], precision=high)
    time_part += jnp.einsum("kas,ast->tk", inner[:, :, rank_two:], core[half:], precision=high)
    chan_slots = jnp.where((jnp.arange(n_channel) == chan_index)[:, None, None], chan_part[None], 0.0)
    time_slots = jnp.where((jnp.arange(n_time) == time_index)[:, None, None], time_part[None], 0.0)
    n_core = core_part.size // 128
    n_chan = n_channel * chan_part.size // 128
    n_rows = n_core + n_chan + n_time * time_part.size // 128
    piece_rows = -(-n_rows // 256) * 8
    packed = jnp.concatenate(
        [
            (core_part / math.sqrt(total_sensors * total_time * total_chan)).reshape(-1, 128),
            (chan_slots / math.sqrt(total_sensors * total_time)).reshape(-1, 128),
            (time_slots / math.sqrt(total_sensors * total_chan)).reshape(-1, 128),
            jnp.zeros((32 * piece_rows - n_rows, 128), f32),
        ],
        axis=0,
    ).reshape(2, 4, 4, piece_rows, 128)
    total, fit_share = sum_all(packed, fit_pack)
    sensor_grad = jnp.concatenate([fit_share[:, :rank_one], fit_share[:, rank_one:]], axis=0)
    total = total.reshape(-1, 128)
    core_sum = total[:n_core].reshape(rank_three, rank_one // 2, 2, rank_two)
    core_grad = core_sum.transpose(2, 1, 3, 0).reshape(rank_one, rank_two, rank_three)
    chan_all = total[n_core : n_core + n_chan].reshape(n_channel, rank_two, chan_rows)
    time_all = total[n_core + n_chan : n_rows].reshape(n_time, rank_three, time_rows)
    channel_grad = lax.dynamic_index_in_dim(chan_all, chan_index, 0, keepdims=False).T
    time_grad = lax.dynamic_index_in_dim(time_all, time_index, 0, keepdims=False).T
    return (core_grad, sensor_grad, channel_grad, time_grad)


def solution(mesh):
    return jax.shard_map(
        on_device,
        mesh=mesh,
        in_specs=(
            P("sensor", "tm", "channel"),
            P(),
            P("sensor", None),
            P("channel", None),
            P("tm", None),
            P("sensor", None),
            P("sensor", None, None, None),
        ),
        out_specs=(P(), P(("sensor", "channel", "tm"), None), P("channel", None), P("tm", None)),
        check_vma=False,
    )
```
